32 devices in a mesh: groups: 2 (over x), expert: 2 (over core), tensor: 8 (over z, y).
Axes of the slice: x: 2, y: 2, z: 4, core: 2. Of those that a mesh axis runs over, the one named last changes fastest.
Arguments:
- tokens: bfloat16 [2048, 3072], P(('groups', 'expert', 'tensor')), parts along dimension 0, may hold values from -6 to 6
- expert_ids: int32 [2048, 1], P(('groups', 'expert', 'tensor')), parts along dimension 0, may hold values from 0 to 1; in each aligned block of 64 rows (0 to 63, 64 to 127, ...) at most 48 rows name the same one
- gates: float32 [2048], P(('groups', 'expert', 'tensor')), parts along dimension 0, may hold values from 0.2 to 1
- gate_weight: bfloat16 [2, 3072, 16384], P('expert', None, 'tensor'), may hold values from -0.109375 to 0.109375
- up_weight: bfloat16 [2, 3072, 16384], P('expert', None, 'tensor'), may hold values from -0.109375 to 0.109375
- down_weight: bfloat16 [2, 16384, 3072], P('expert', 'tensor'), may hold values from -0.046875 to 0.046875
Outputs:
- routed: bfloat16 [2048, 3072], P(('groups', 'expert', 'tensor')), parts along dimension 0
The draws below stay inside these ranges and needn't reach their ends.
There are 2 independent parts, one for each index of `groups`. The reference program is written for one: setup_inputs(seed, part) draws one part's arguments, and reference() takes and returns one part's arrays. A program takes and returns all parts, laid end to end along the dimension named above; an argument that names none is the same for every part. Nothing has to cross between parts.
Inputs may be any that keep to these rules, and one draw needn't show every extreme that they name: `expert_ids`: among the 64 rows of one device no expert is named more than 48 times; in every draw some device names one expert exactly 48 times.
All inputs are finite; a program needn't handle non-finite values.
Results may differ from the reference program's by a relative error of at most 0.014.
Values may be sent and summed in bfloat16 or wider, within the bound.
A program may use at most 128 MiB of HBM per device.

```python
import math
import jax
import jax.numpy as jnp
import numpy as np

D = 3072
FF = 16384
ROWS_DEV = 64
CAP = 48
EXPERTS = 2
ROWS = 1024
N_TENSOR = 8


def block_levels(stream_key, shape, cuts, low, largest):
    factor_of, own = 1.0, jax.random.fold_in(stream_key, 6)
    for dim, blocks in cuts:
        steps = jnp.exp(jax.random.uniform(jax.random.fold_in(own, dim), (blocks,), jnp.float32, low / len(cuts), largest / len(cuts)))
        factor_of = factor_of * jnp.repeat(steps, shape[dim] // blocks).reshape([-1 if axis == dim else 1 for axis in range(len(shape))])
    return factor_of


def assign_block(stream_key, own, number, rows, amount, top, reach, skew):
    ranking = jax.random.permutation(stream_key, amount)
    crowded, ordinary = load_shares(amount, rows * top, reach, skew, True), load_shares(amount, rows * top, reach, skew, False)
    places = jnp.arange(amount)

    def named(tallies, offset_by):
        used = int((tallies > 0).sum())
        fixed = max(1, used // 4)
        shifted = fixed + (places - fixed + offset_by * (used - fixed)) % max(1, amount - fixed)
        return jnp.zeros((amount,), jnp.int32).at[ranking[jnp.where(places < fixed, places, shifted)]].set(jnp.asarray(tallies, jnp.int32))

    tallies = jnp.where(number % 4 == 0, named(crowded, number // 4), named(ordinary, number - number // 4 - 1))
    mixed = jax.random.permutation(jax.random.fold_in(own, 3), amount)
    giver, receiver = mixed[0:amount // 2 * 2:2], mixed[1:amount // 2 * 2:2]
    room = jnp.minimum(tallies[giver] - 1, reach - tallies[receiver]) // 2
    room = jnp.where((giver == ranking[0]) | (receiver == ranking[0]) | (tallies[receiver] == 0), 0, jnp.maximum(room, 0))
    shifted = jax.random.randint(jax.random.fold_in(own, 4), (amount // 2,), 0, 1 << 20) % (room + 1)
    tallies = tallies.at[giver].add(-shifted).at[receiver].add(shifted)
    labels = jnp.searchsorted(jnp.cumsum(tallies), jnp.arange(rows * top), side="right").astype(jnp.int32)
    grid = labels.reshape(top, rows).T
    grid = grid[jax.random.permutation(jax.random.fold_in(own, 1), rows)]
    offset_by = jax.random.randint(jax.random.fold_in(own, 2), (rows, 1), 0, top)
    return jnp.take_along_axis(grid, (jnp.arange(top)[None, :] + offset_by) % top, axis=1)


def load_shares(number_of, total, most, skew, full):
    portions = [(1 << 20) // math.isqrt(standing ** skew) + 1 for standing in range(1, number_of + 1)]
    largest = most if full else min(most, max(-(-total // number_of), total * portions[0] // sum(portions)))
    least = 1 if total - largest >= number_of - 1 else 0
    counts, surplus = [largest] + [least] * (number_of - 1), total - largest - least * (number_of - 1)
    while surplus > 0:
        free = [i for i in range(1, number_of) if counts[i] < largest] or [i for i in range(1, number_of) if counts[i] < most]
        whole, left = sum([portions[i] for i in free]), surplus
        for i in free:
            more = min(most - counts[i], max(1, left * portions[i] // whole), surplus)
            counts[i] = counts[i] + more
            surplus = surplus - more
    return np.array(counts)


def gaussian(key, dims, spread, limit, pieces=(), kind=jnp.bfloat16):
    level = block_levels(key, dims, pieces, -0.22, 0.18) if pieces else 1.0
    array = jax.random.normal(key, dims, jnp.float32) * spread * level
    return jnp.minimum(jnp.maximum(array, -limit), limit).astype(kind)


def setup_inputs(seed: int = 0, part: int = 0) -> dict:
    keys = jax.random.split(jax.random.key(seed), 7)
    part_splits = jax.random.split(jax.random.fold_in(keys[6], part), 7)
    tokens = gaussian(part_splits[0], (ROWS, D), 1.0, 6.0, ((0, 16),))
    expert_ids_keys = jax.random.split(jax.random.fold_in(part_splits[1], 1), ROWS // ROWS_DEV)
    expert_ids_turns = jax.random.permutation(jax.random.fold_in(part_splits[1], 3), ROWS // ROWS_DEV)
    expert_ids = jax.vmap(lambda own, number: assign_block(jax.random.fold_in(part_splits[1], 2), own, number, ROWS_DEV, EXPERTS, 1, CAP, 1))(expert_ids_keys, expert_ids_turns).reshape((ROWS, 1))
    gates = jnp.clip(0.2 + 0.8 * jax.random.uniform(part_splits[2], (ROWS,), jnp.float32) ** block_levels(part_splits[2], (ROWS,), ((0, 16),), -0.2, 0.2), 0.2, 1.0)
    gate_weight = gaussian(keys[3], (EXPERTS, D, FF), D ** -0.5, 0.109375, ((0, 2), (2, 8)))
    up_weight = gaussian(keys[4], (EXPERTS, D, FF), D ** -0.5, 0.109375, ((0, 2), (2, 8)))
    down_weight = gaussian(keys[5], (EXPERTS, FF, D), FF ** -0.5, 0.046875, ((0, 2), (1, 8)))
    return {"tokens": tokens, "expert_ids": expert_ids, "gates": gates, "gate_weight": gate_weight, "up_weight": up_weight, "down_weight": down_weight}


def reference(tokens, expert_ids, gates, gate_weight, up_weight, down_weight):
    experts = gate_weight.shape[0]
    width = tokens.shape[1]
    hidden_units = gate_weight.shape[2]
    block = hidden_units // N_TENSOR
    sources = tokens.shape[0] // ROWS_DEV
    expert_of = expert_ids[:, 0].reshape(sources, ROWS_DEV)
    matches = (expert_of[:, :, None] == jnp.arange(experts, dtype=jnp.int32)[None, None, :]).astype(jnp.int32)
    earlier = jnp.cumsum(matches, axis=1) - matches
    position = jnp.sum(earlier * matches, axis=2).astype(jnp.int32)
    column = (expert_of * CAP + position).astype(jnp.int32)
    slot_table = (column[:, :, None] == jnp.arange(experts * CAP, dtype=jnp.int32)[None, None, :]).astype(jnp.float32)
    blocks = tokens.reshape(sources, ROWS_DEV, width).astype(jnp.float32)
    buffers = jnp.einsum("srj,srd->jsd", slot_table, blocks).reshape(experts, CAP * sources, width)
    outputs = []
    for expert in range(experts):
        arrived = buffers[expert].astype(jnp.bfloat16)
        gate_pre = jnp.dot(arrived, gate_weight[expert], preferred_element_type=jnp.float32)
        up_pre = jnp.dot(arrived, up_weight[expert], preferred_element_type=jnp.float32)
        hidden = (jax.nn.gelu(gate_pre, approximate=True) * up_pre).astype(jnp.bfloat16)
        total = jnp.zeros((arrived.shape[0], width), jnp.float32)
        for piece in range(N_TENSOR):
            part = jnp.dot(hidden[:, piece * block:(piece + 1) * block], down_weight[expert, piece * block:(piece + 1) * block, :], preferred_element_type=jnp.float32)
            total = total + part.astype(jnp.bfloat16).astype(jnp.float32)
        outputs.append(total.astype(jnp.bfloat16))
    stacked = jnp.stack(outputs).reshape(experts, CAP, sources, width)
    stacked = jnp.transpose(stacked, (2, 0, 1, 3)).reshape(sources, experts * CAP, width).astype(jnp.float32)
    picked = jnp.einsum("srj,sjd->srd", slot_table, stacked).reshape(sources * ROWS_DEV, width)
    return (picked * gates[:, None]).astype(jnp.bfloat16)
```

```python
import jax
import jax.numpy as jnp
from jax import lax
from jax.sharding import PartitionSpec as P

CAP = 48
IN_CHUNKS = 1
OUT_CHUNKS = 2


def slot_table(expert_ids, experts):
    expert_of = expert_ids[:, 0]
    matches = (expert_of[:, None] == jnp.arange(experts, dtype=jnp.int32)[None, :]).astype(
        jnp.int32
    )
    earlier = jnp.cumsum(matches, axis=0) - matches
    position = jnp.sum(earlier * matches, axis=1)
    column = expert_of * CAP + position
    return (column[:, None] == jnp.arange(experts * CAP, dtype=jnp.int32)[None, :]).astype(
        jnp.bfloat16
    )


def per_device(tokens, expert_ids, gates, gate_weight, up_weight, down_weight):
    rows, width = tokens.shape
    experts = lax.axis_size("expert") * gate_weight.shape[0]
    tensor_size = lax.axis_size("tensor")
    group_ids = lax.all_gather(expert_ids, "tensor", axis=0, tiled=True)
    tables = jax.vmap(slot_table, in_axes=(0, None))(group_ids.reshape(tensor_size, rows, 1), experts)

    gate_pre, up_pre = None, None
    step = width // IN_CHUNKS
    for chunk in range(IN_CHUNKS):
        cut = slice(chunk * step, (chunk + 1) * step)
        gathered = lax.all_gather(tokens[:, cut], "tensor", axis=0)
        outgoing = jnp.einsum("trj,trd->tjd", tables, gathered, preferred_element_type=jnp.float32)
        outgoing = outgoing.astype(jnp.bfloat16).reshape(tensor_size, experts, CAP, step)
        arrived = lax.all_to_all(
            outgoing, "expert", split_axis=1, concat_axis=1, tiled=True
        ).reshape(tensor_size * experts * CAP, step)
        gate_part = jnp.dot(arrived, gate_weight[0, cut], preferred_element_type=jnp.float32)
        up_part = jnp.dot(arrived, up_weight[0, cut], preferred_element_type=jnp.float32)
        gate_pre = gate_part if gate_pre is None else gate_pre + gate_part
        up_pre = up_part if up_pre is None else up_pre + up_part
    hidden = (jax.nn.gelu(gate_pre, approximate=True) * up_pre).astype(jnp.bfloat16)

    step = width // OUT_CHUNKS
    pieces = []
    for chunk in range(OUT_CHUNKS):
        cut = slice(chunk * step, (chunk + 1) * step)
        product = jnp.dot(hidden, down_weight[0, :, cut], preferred_element_type=jnp.float32)
        product = product.astype(jnp.bfloat16).reshape(tensor_size, experts, CAP, step)
        returned = lax.all_to_all(
            product, "expert", split_axis=1, concat_axis=1, tiled=True
        ).reshape(tensor_size, experts * CAP, step)
        placed = jnp.einsum("trj,tjd->trd", tables, returned, preferred_element_type=jnp.float32)
        placed = placed.astype(jnp.bfloat16).reshape(tensor_size * rows, step)
        summed = lax.psum_scatter(placed, "tensor", scatter_dimension=0, tiled=True)
        pieces.append((summed.astype(jnp.float32) * gates[:, None]).astype(jnp.bfloat16))
    return jnp.concatenate(pieces, axis=1) if len(pieces) > 1 else pieces[0]


def solution(mesh):
    return jax.shard_map(
        per_device,
        mesh=mesh,
        in_specs=(
            P(("groups", "expert", "tensor"), None),
            P(("groups", "expert", "tensor"), None),
            P(("groups", "expert", "tensor")),
            P("expert", None, "tensor"),
            P("expert", None, "tensor"),
            P("expert", "tensor", None),
        ),
        out_specs=P(("groups", "expert", "tensor"), None),
        check_vma=False,
    )
```

```python
import functools

import jax
import jax.numpy as jnp
from jax import lax
from jax.experimental import pallas as pl
from jax.experimental.pallas import tpu as pltpu
from jax.sharding import PartitionSpec as P

CAP = 48
LANES = 128
STREAMS = 4


def place_of(zigzag, size, index):
    if not zigzag:
        return index
    odd = index % 2
    return (1 - odd) * (index // 2) + odd * (size - 1 - index // 2)


def index_of(zigzag, size, place):
    place = (place + 2 * size) % size
    if not zigzag:
        return place
    back = place // (size // 2)
    return (1 - back) * (2 * place) + back * (2 * (size - 1 - place) + 1)


def greet(zigzag, size, place):
    barrier = pltpu.get_barrier_semaphore()
    for way in (1, -1):
        pl.semaphore_signal(
            barrier,
            inc=1,
            device_id={"tensor": index_of(zigzag, size, place + way)},
            device_id_type=pl.DeviceIdType.MESH,
        )
    pl.semaphore_wait(barrier, 2)


def send(zigzag, size, place, way, source, target, send_sem, recv_sem):
    return pltpu.make_async_remote_copy(
        src_ref=source,
        dst_ref=target,
        send_sem=send_sem,
        recv_sem=recv_sem,
        device_id={"tensor": index_of(zigzag, size, place + way)},
        device_id_type=pl.DeviceIdType.MESH,
    )


def gather_kernel(zigzag, size, tokens, column, all_tokens, all_columns, send_sem, recv_sem):
    me = lax.axis_index("tensor")
    place = place_of(zigzag, size, me)
    greet(zigzag, size, place)
    part = tokens.shape[1] // STREAMS
    streams = [(column, all_columns, slice(0, LANES), 1)]
    for number in range(STREAMS):
        cut = slice(number * part, (number + 1) * part)
        streams.append((tokens, all_tokens, cut, 1 - 2 * (number % 2)))
    copies = {}
    for step in range(size - 1):
        for number, (mine, whole, cut, way) in enumerate(streams):
            owner = index_of(zigzag, size, place - way * step)
            target = whole.at[owner, :, cut]
            source = mine.at[:, cut]
            if step:
                copies[step - 1, number].wait_recv()
                source = target
            copies[step, number] = send(
                zigzag, size, place, way, source, target,
                send_sem.at[step, number], recv_sem.at[step, number],
            )
            copies[step, number].start()
        if step == 0:
            all_tokens[me] = tokens[...]
            all_columns[me] = column[...]
    for number in range(len(streams)):
        copies[size - 2, number].wait_recv()
    for copy in copies.values():
        copy.wait_send()


def reduce_kernel(zigzag, size, terms, out, held, send_sem, recv_sem):
    me = lax.axis_index("tensor")
    place = place_of(zigzag, size, me)
    greet(zigzag, size, place)
    part = terms.shape[2] // STREAMS
    copies = {}
    for step in range(size):
        for number in range(STREAMS):
            cut = slice(number * part, (number + 1) * part)
            way = 1 - 2 * (number % 2)
            owner = index_of(zigzag, size, place - way * (1 + step))
            source = terms.at[owner, :, cut]
            if step:
                copies[step - 1, number].wait_recv()
                total = held[step - 1, number].astype(jnp.float32) + terms[
                    owner, :, cut
                ].astype(jnp.float32)
                if step == size - 1:
                    out[:, cut] = total.astype(out.dtype)
                    continue
                held[step - 1, number] = total.astype(held.dtype)
                source = held.at[step - 1, number]
            copies[step, number] = send(
                zigzag, size, place, way, source, held.at[step, number],
                send_sem.at[step, number], recv_sem.at[step, number],
            )
            copies[step, number].start()
    for copy in copies.values():
        copy.wait_send()


def ring_gather(zigzag, tokens, column):
    size = lax.axis_size("tensor")
    vmem = pl.BlockSpec(memory_space=pltpu.VMEM)
    sems = pltpu.SemaphoreType.DMA((size - 1, STREAMS + 1))
    return pl.pallas_call(
        functools.partial(gather_kernel, zigzag, size),
        out_shape=(
            jax.ShapeDtypeStruct((size, *tokens.shape), tokens.dtype),
            jax.ShapeDtypeStruct((size, *column.shape), column.dtype),
        ),
        in_specs=[vmem, vmem],
        out_specs=(vmem, vmem),
        scratch_shapes=[sems, sems],
        compiler_params=pltpu.CompilerParams(collective_id=0, has_side_effects=True),
        name="ring_gather",
    )(tokens, column)


def ring_reduce(zigzag, terms):
    size, rows, width = terms.shape
    vmem = pl.BlockSpec(memory_space=pltpu.VMEM)
    sems = pltpu.SemaphoreType.DMA((size - 1, STREAMS))
    return pl.pallas_call(
        functools.partial(reduce_kernel, zigzag, size),
        out_shape=jax.ShapeDtypeStruct((rows, width), terms.dtype),
        in_specs=[vmem],
        out_specs=vmem,
        scratch_shapes=[
            pltpu.VMEM((size - 1, STREAMS, rows, width // STREAMS), terms.dtype),
            sems,
            sems,
        ],
        compiler_params=pltpu.CompilerParams(collective_id=1, has_side_effects=True),
        name="ring_reduce",
    )(terms)


def slot_of(expert_ids, experts):
    expert_of = expert_ids[:, 0]
    matches = (expert_of[:, None] == jnp.arange(experts, dtype=jnp.int32)[None, :]).astype(
        jnp.int32
    )
    earlier = jnp.cumsum(matches, axis=0) - matches
    position = jnp.sum(earlier * matches, axis=1)
    return expert_of * CAP + position


def per_device(zigzag, tokens, expert_ids, gates, gate_weight, up_weight, down_weight):
    rows, width = tokens.shape
    experts = lax.axis_size("expert") * gate_weight.shape[0]
    size = lax.axis_size("tensor")
    column = jnp.broadcast_to(
        slot_of(expert_ids, experts).astype(jnp.bfloat16)[:, None], (rows, LANES)
    )
    gathered, columns = ring_gather(zigzag, tokens, column)
    slots = jnp.arange(experts * CAP, dtype=jnp.float32)
    tables = (columns[:, :, :1].astype(jnp.float32) == slots).astype(jnp.bfloat16)

    outgoing = jnp.einsum("trj,trd->tjd", tables, gathered, preferred_element_type=jnp.float32)
    outgoing = outgoing.astype(jnp.bfloat16).reshape(size, experts, CAP, width)
    arrived = lax.all_to_all(
        outgoing, "expert", split_axis=1, concat_axis=1, tiled=True
    ).reshape(size * experts * CAP, width)
    gate_pre = jnp.dot(arrived, gate_weight[0], preferred_element_type=jnp.float32)
    up_pre = jnp.dot(arrived, up_weight[0], preferred_element_type=jnp.float32)
    hidden = (jax.nn.gelu(gate_pre, approximate=True) * up_pre).astype(jnp.bfloat16)

    product = jnp.dot(hidden, down_weight[0], preferred_element_type=jnp.float32)
    product = product.astype(jnp.bfloat16).reshape(size, experts, CAP, width)
    returned = lax.all_to_all(
        product, "expert", split_axis=1, concat_axis=1, tiled=True
    ).reshape(size, experts * CAP, width)
    placed = jnp.einsum("trj,tjd->trd", tables, returned, preferred_element_type=jnp.float32)
    summed = ring_reduce(zigzag, placed.astype(jnp.bfloat16))
    return (summed.astype(jnp.float32) * gates[:, None]).astype(jnp.bfloat16)


def folds(mesh):
    names = mesh.axis_names
    line = mesh.devices.transpose(
        [names.index("groups"), names.index("expert"), names.index("tensor")]
    )[0, 0]
    coords = [getattr(device, "coords", None) for device in line[:2]]
    return line.size % 2 == 0 and (coords[0] is None or coords[0][2] == coords[1][2])


def solution(mesh):
    return jax.shard_map(
        functools.partial(per_device, folds(mesh)),
        mesh=mesh,
        in_specs=(
            P(("groups", "expert", "tensor"), None),
            P(("groups", "expert", "tensor"), None),
            P(("groups", "expert", "tensor")),
            P("expert", None, "tensor"),
            P("expert", None, "tensor"),
            P("expert", "tensor", None),
        ),
        out_specs=P(("groups", "expert", "tensor"), None),
        check_vma=False,
    )
```

```python
import functools

import jax
import jax.numpy as jnp
from jax import lax
from jax.experimental import pallas as pl
from jax.experimental.pallas import tpu as pltpu
from jax.sharding import PartitionSpec as P

CAP = 48
LANES = 128
STREAMS = 4


def place_of(zigzag, size, index):
    if not zigzag:
        return index
    odd = index % 2
    return (1 - odd) * (index // 2) + odd * (size - 1 - index // 2)


def index_of(zigzag, size, place):
    place = (place + 2 * size) % size
    if not zigzag:
        return place
    back = place // (size // 2)
    return (1 - back) * (2 * place) + back * (2 * (size - 1 - place) + 1)


def greet(zigzag, size, place):
    barrier = pltpu.get_barrier_semaphore()
    for way in (1, -1):
        pl.semaphore_signal(
            barrier,
            inc=1,
            device_id={"tensor": index_of(zigzag, size, place + way)},
            device_id_type=pl.DeviceIdType.MESH,
        )
    pl.semaphore_wait(barrier, 2)


def send(zigzag, size, place, way, source, target, send_sem, recv_sem):
    return pltpu.make_async_remote_copy(
        src_ref=source,
        dst_ref=target,
        send_sem=send_sem,
        recv_sem=recv_sem,
        device_id={"tensor": index_of(zigzag, size, place + way)},
        device_id_type=pl.DeviceIdType.MESH,
    )


def gather_kernel(zigzag, size, tokens, column, all_tokens, all_columns, send_sem, recv_sem):
    me = lax.axis_index("tensor")
    place = place_of(zigzag, size, me)
    greet(zigzag, size, place)
    part = tokens.shape[1] // STREAMS
    streams = [(column, all_columns, slice(0, LANES), 1)]
    for number in range(STREAMS):
        cut = slice(number * part, (number + 1) * part)
        streams.append((tokens, all_tokens, cut, 1 - 2 * (number % 2)))
    copies = {}
    for step in range(size - 1):
        for number, (mine, whole, cut, way) in enumerate(streams):
            owner = index_of(zigzag, size, place - way * step)
            target = whole.at[owner, :, cut]
            source = mine.at[:, cut]
            if step:
                copies[step - 1, number].wait_recv()
                source = target
            copies[step, number] = send(
                zigzag, size, place, way, source, target,
                send_sem.at[step, number], recv_sem.at[step, number],
            )
            copies[step, number].start()
        if step == 0:
            all_tokens[me] = tokens[...]
            all_columns[me] = column[...]
    for number in range(len(streams)):
        copies[size - 2, number].wait_recv()
    for copy in copies.values():
        copy.wait_send()


def reduce_kernel(zigzag, size, terms, out, held, send_sem, recv_sem):
    me = lax.axis_index("tensor")
    place = place_of(zigzag, size, me)
    greet(zigzag, size, place)
    part = terms.shape[2] // STREAMS
    copies = {}
    for step in range(size):
        for number in range(STREAMS):
            cut = slice(number * part, (number + 1) * part)
            way = 1 - 2 * (number % 2)
            owner = index_of(zigzag, size, place - way * (1 + step))
            source = terms.at[owner, :, cut]
            if step:
                copies[step - 1, number].wait_recv()
                total = held[step - 1, number].astype(jnp.float32) + terms[
                    owner, :, cut
                ].astype(jnp.float32)
                if step == size - 1:
                    out[:, cut] = total.astype(out.dtype)
                    continue
                held[step - 1, number] = total.astype(held.dtype)
                source = held.at[step - 1, number]
            copies[step, number] = send(
                zigzag, size, place, way, source, held.at[step, number],
                send_sem.at[step, number], recv_sem.at[step, number],
            )
            copies[step, number].start()
    for copy in copies.values():
        copy.wait_send()


def ring_gather(zigzag, tokens, column):
    size = lax.axis_size("tensor")
    vmem = pl.BlockSpec(memory_space=pltpu.VMEM)
    sems = pltpu.SemaphoreType.DMA((size - 1, STREAMS + 1))
    return pl.pallas_call(
        functools.partial(gather_kernel, zigzag, size),
        out_shape=(
            jax.ShapeDtypeStruct((size, *tokens.shape), tokens.dtype),
            jax.ShapeDtypeStruct((size, *column.shape), column.dtype),
        ),
        in_specs=[vmem, vmem],
        out_specs=(vmem, vmem),
        scratch_shapes=[sems, sems],
        compiler_params=pltpu.CompilerParams(collective_id=0, has_side_effects=True),
        name="ring_gather",
    )(tokens, column)


def ring_reduce(zigzag, terms):
    size, rows, width = terms.shape
    vmem = pl.BlockSpec(memory_space=pltpu.VMEM)
    sems = pltpu.SemaphoreType.DMA((size - 1, STREAMS))
    return pl.pallas_call(
        functools.partial(reduce_kernel, zigzag, size),
        out_shape=jax.ShapeDtypeStruct((rows, width), terms.dtype),
        in_specs=[vmem],
        out_specs=vmem,
        scratch_shapes=[
            pltpu.VMEM((size - 1, STREAMS, rows, width // STREAMS), terms.dtype),
            sems,
            sems,
        ],
        compiler_params=pltpu.CompilerParams(collective_id=1, has_side_effects=True),
        name="ring_reduce",
    )(terms)


def slot_of(expert_ids, experts):
    expert_of = expert_ids[:, 0]
    matches = (expert_of[:, None] == jnp.arange(experts, dtype=jnp.int32)[None, :]).astype(
        jnp.int32
    )
    earlier = jnp.cumsum(matches, axis=0) - matches
    position = jnp.sum(earlier * matches, axis=1)
    return expert_of * CAP + position


def per_device(zigzag, tokens, expert_ids, gates, gate_weight, up_weight, down_weight):
    rows, width = tokens.shape
    experts = lax.axis_size("expert") * gate_weight.shape[0]
    size = lax.axis_size("tensor")
    column = jnp.broadcast_to(
        slot_of(expert_ids, experts).astype(jnp.bfloat16)[:, None], (rows, LANES)
    )
    gathered, columns = ring_gather(zigzag, tokens, column)
    here = lax.axis_index("expert")
    slots = jnp.arange(CAP, dtype=jnp.float32)
    numbers = columns[:, :, :1].astype(jnp.float32)
    own_table, away_table = (
        (numbers == slots + (expert * CAP).astype(jnp.float32)).astype(jnp.bfloat16)
        for expert in (here, 1 - here)
    )
    swap = [(0, 1), (1, 0)]

    def packed(table):
        rows_of = jnp.einsum("trj,trd->tjd", table, gathered, preferred_element_type=jnp.float32)
        return rows_of.astype(jnp.bfloat16).reshape(size * CAP, width)

    def hidden_of(arrived):
        gate_pre = jnp.dot(arrived, gate_weight[0], preferred_element_type=jnp.float32)
        up_pre = jnp.dot(arrived, up_weight[0], preferred_element_type=jnp.float32)
        return (jax.nn.gelu(gate_pre, approximate=True) * up_pre).astype(jnp.bfloat16)

    def partial_of(hidden):
        product = jnp.dot(hidden, down_weight[0], preferred_element_type=jnp.float32)
        return product.astype(jnp.bfloat16)

    arrived = lax.ppermute(packed(away_table), "expert", swap)
    own_hidden = hidden_of(packed(own_table))
    returned = lax.ppermute(partial_of(hidden_of(arrived)), "expert", swap)
    kept = partial_of(own_hidden)
    placed = sum(
        jnp.einsum(
            "trj,tjd->trd", table, part.reshape(size, CAP, width),
            preferred_element_type=jnp.float32,
        )
        for table, part in ((own_table, kept), (away_table, returned))
    )
    summed = ring_reduce(zigzag, placed.astype(jnp.bfloat16))
    return (summed.astype(jnp.float32) * gates[:, None]).astype(jnp.bfloat16)


def folds(mesh):
    names = mesh.axis_names
    line = mesh.devices.transpose(
        [names.index("groups"), names.index("expert"), names.index("tensor")]
    )[0, 0]
    coords = [getattr(device, "coords", None) for device in line[:2]]
    return line.size % 2 == 0 and (coords[0] is None or coords[0][2] == coords[1][2])


def solution(mesh):
    return jax.shard_map(
        functools.partial(per_device, folds(mesh)),
        mesh=mesh,
        in_specs=(
            P(("groups", "expert", "tensor"), None),
            P(("groups", "expert", "tensor"), None),
            P(("groups", "expert", "tensor")),
            P("expert", None, "tensor"),
            P("expert", None, "tensor"),
            P("expert", "tensor", None),
        ),
        out_specs=P(("groups", "expert", "tensor"), None),
        check_vma=False,
    )
```
